32 devices in a mesh: groups: 2 (over x), expert: 8 (over z, y), helper: 2 (over core).
Axes of the slice: x: 2, y: 2, z: 4, core: 2. Of those that a mesh axis runs over, the one named last changes fastest.
Arguments:
- slot_rows: bfloat16 [12288, 4096], P(('groups', 'expert', 'helper')), parts along dimension 0, may hold values from -6 to 6
- experts: int32 [3072, 2], P(('groups', 'expert', 'helper')), parts along dimension 0, may hold values from 0 to 7, all different within a row; in each aligned block of 96 rows (0 to 95, 96 to 191, ...) at most 48 rows name the same one
- gate_values: float32 [3072, 2], P(('groups', 'expert', 'helper')), parts along dimension 0, may hold values from 0.1 to 1
- gate_weight: bfloat16 [8, 4096, 768], P('expert', None, 'helper'), may hold values from -0.09375 to 0.09375
- up_weight: bfloat16 [8, 4096, 768], P('expert', None, 'helper'), may hold values from -0.09375 to 0.09375
- down_weight: bfloat16 [8, 768, 4096], P('expert', 'helper'), may hold values from -0.21875 to 0.21875
Outputs:
- layer_output: bfloat16 [3072, 4096], P(('groups', 'expert', 'helper')), parts along dimension 0
The draws below stay inside these ranges and needn't reach their ends.
There are 2 independent parts, one for each index of `groups`. The reference program is written for one: setup_inputs(seed, part) draws one part's arguments, and reference() takes and returns one part's arrays. A program takes and returns all parts, laid end to end along the dimension named above; an argument that names none is the same for every part. Nothing has to cross between parts.
Inputs may be any that keep to these rules, and one draw needn't show every extreme that they name: Each row names 2 different experts. Within the rows of one token block no expert is named by more than 48 rows, and in some block one expert is named by exactly 48 rows. Every expert is named by some row.
All inputs are finite; a program needn't handle non-finite values.
Results may differ from the reference program's by a relative error of at most 0.0058.
Values may be sent and summed in bfloat16 or wider, within the bound.
A program may use at most 128 MiB of HBM per device.

```python
import math
import jax
import jax.numpy as jnp
import numpy as np
from jax import lax

D = 4096
FF = 768
TOPK = 2
TOK_DEV = 96
EXPERTS = 8
TOKENS = 1536
M = 48
CAP = 768
N_EXPERT = 8
N_HELPER = 2


def level_of(key, shape, split, least, top_value):
    loudness = 1.0
    for dim, blocks in split:
        draws = jax.random.uniform(jax.random.fold_in(jax.random.fold_in(key, 6), dim), (blocks,), jnp.float32, least / len(split), top_value / len(split))
        loudness = loudness * jnp.repeat(jnp.exp(draws), shape[dim] // blocks).reshape((-1,) + (1,) * (len(shape) - 1 - dim))
    return loudness


def deal_out(own_key, own, number, rows, amount, top, most, skew):
    order = jax.random.permutation(own_key, amount)
    packed, common = portions_of(amount, rows * top, most, skew, True), portions_of(amount, rows * top, most, skew, False)
    places = jnp.arange(amount)

    def named(tallies, rotation):
        used = int((tallies > 0).sum())
        fixed = max(1, used // 4)
        passed = fixed + (places - fixed + rotation * (used - fixed)) % max(1, amount - fixed)
        return jnp.zeros((amount,), jnp.int32).at[order[jnp.where(places < fixed, places, passed)]].set(jnp.asarray(tallies, jnp.int32))

    tallies = jnp.where(number % 4 == 0, named(packed, number // 4), named(common, number - number // 4 - 1))
    mixed = jax.random.permutation(jax.random.fold_in(own, 3), amount)
    donor, taker = mixed[0:amount // 2 * 2:2], mixed[1:amount // 2 * 2:2]
    margin = jnp.minimum(tallies[donor] - 1, most - tallies[taker]) // 2
    margin = jnp.where((donor == order[0]) | (taker == order[0]) | (tallies[taker] == 0), 0, jnp.maximum(margin, 0))
    passed = jax.random.randint(jax.random.fold_in(own, 4), (amount // 2,), 0, 1 << 20) % (margin + 1)
    tallies = tallies.at[donor].add(-passed).at[taker].add(passed)
    labels = jnp.searchsorted(jnp.cumsum(tallies), jnp.arange(rows * top), side="right").astype(jnp.int32)
    listing = labels.reshape(top, rows).T
    listing = listing[jax.random.permutation(jax.random.fold_in(own, 1), rows)]
    rotation = jax.random.randint(jax.random.fold_in(own, 2), (rows, 1), 0, top)
    return jnp.take_along_axis(listing, (jnp.arange(top)[None, :] + rotation) % top, axis=1)


def portions_of(number_of, total, limit, skew, full):
    weights = [(1 << 20) // math.isqrt(grade ** skew) + 1 for grade in range(1, number_of + 1)]
    largest = limit if full else min(limit, max(-(-total // number_of), total * weights[0] // sum(weights)))
    least = 1 if total - largest >= number_of - 1 else 0
    holding, spare = [largest] + [least] * (number_of - 1), total - largest - least * (number_of - 1)
    while spare > 0:
        free = [i for i in range(1, number_of) if holding[i] < largest] or [i for i in range(1, number_of) if holding[i] < limit]
        whole, left = sum([weights[i] for i in free]), spare
        for i in free:
            addition = min(limit - holding[i], max(1, left * weights[i] // whole), spare)
            holding[i] = holding[i] + addition
            spare = spare - addition
    return np.array(holding)


def centred(own_key, dims, width, most, cuts=(), held_as=jnp.bfloat16):
    gain = level_of(own_key, dims, cuts, -0.22, 0.18) if cuts else 1.0
    values = jax.random.normal(own_key, dims, jnp.float32) * width * gain
    return jnp.minimum(jnp.maximum(values, -most), most).astype(held_as)


def setup_inputs(seed: int = 0, part: int = 0) -> dict:
    streams_of = jax.random.split(jax.random.key(seed), 7)
    part_splits = jax.random.split(jax.random.fold_in(streams_of[6], part), 7)
    slot_rows = centred(part_splits[0], (EXPERTS * CAP, D), 1.0, 6.0, ((0, 16),))
    experts_keys = jax.random.split(jax.random.fold_in(part_splits[1], 1), TOKENS // TOK_DEV)
    experts_turns = jax.random.permutation(jax.random.fold_in(part_splits[1], 3), TOKENS // TOK_DEV)
    experts = jax.vmap(lambda own, number: deal_out(jax.random.fold_in(part_splits[1], 2), own, number, TOK_DEV, EXPERTS, TOPK, M, 2))(experts_keys, experts_turns).reshape((TOKENS, TOPK))
    gate_values = jnp.clip(0.1 + 0.9 * jax.random.uniform(part_splits[2], (TOKENS, TOPK), jnp.float32) ** level_of(part_splits[2], (TOKENS, TOPK), ((0, 16),), -0.2, 0.2), 0.1, 1.0)
    gate_weight = centred(streams_of[3], (EXPERTS, D, FF), D ** -0.5, 0.09375, ((0, 8), (2, 2)))
    up_weight = centred(streams_of[4], (EXPERTS, D, FF), D ** -0.5, 0.09375, ((0, 8), (2, 2)))
    down_weight = centred(streams_of[5], (EXPERTS, FF, D), FF ** -0.5, 0.21875, ((0, 8), (1, 2)))
    return dict(slot_rows=slot_rows, experts=experts, gate_values=gate_values, gate_weight=gate_weight, up_weight=up_weight, down_weight=down_weight)


def slot_numbers(experts):
    blocks = TOKENS // TOK_DEV
    grouped = experts.reshape(blocks, TOK_DEV, TOPK).astype(jnp.int32)
    onehot = (grouped[:, :, :, None] == jnp.arange(EXPERTS, dtype=jnp.int32)[None, None, None, :]).astype(jnp.int32)
    per_token = jnp.sum(onehot, axis=2).astype(jnp.int32)
    before = (jnp.cumsum(per_token, axis=1).astype(jnp.int32) - per_token).astype(jnp.int32)
    within = jnp.take_along_axis(before, grouped, axis=2).astype(jnp.int32)
    block_index = jnp.arange(blocks, dtype=jnp.int32)[:, None, None]
    source_block = (block_index % N_HELPER) * N_EXPERT + block_index // N_HELPER
    placed = grouped * CAP + source_block * M + within
    return placed.reshape(TOKENS, TOPK).astype(jnp.int32)


def expert_block(operands):
    inputs, gate_part, up_part, down_part = operands
    gated = jnp.dot(inputs, gate_part, preferred_element_type=jnp.float32)
    lifted = jnp.dot(inputs, up_part, preferred_element_type=jnp.float32)
    hidden = (jax.nn.silu(gated) * lifted).astype(jnp.bfloat16)
    return jnp.dot(hidden, down_part, preferred_element_type=jnp.float32).astype(jnp.bfloat16)


def reference(slot_rows, experts, gate_values, gate_weight, up_weight, down_weight):
    grouped_rows = slot_rows.reshape(EXPERTS, CAP, D)
    outputs = lax.map(expert_block, (grouped_rows, gate_weight, up_weight, down_weight))
    flattened = outputs.reshape(EXPERTS * CAP, D)
    picked = flattened[slot_numbers(experts)]
    combined = jnp.sum(gate_values[:, :, None] * picked.astype(jnp.float32), axis=1)
    return combined.astype(jnp.bfloat16)
```

```python
import functools
import jax
import jax.numpy as jnp
from jax import lax
from jax.experimental import pallas as pl
from jax.experimental.pallas import tpu as pltpu
from jax.sharding import PartitionSpec as P

COLUMNS = 2
MESH = pl.DeviceIdType.MESH


def remote(src, dst, send, recv, **where):
    return pltpu.make_async_remote_copy(
        src_ref=src, dst_ref=dst, send_sem=send, recv_sem=recv,
        device_id=where, device_id_type=MESH,
    )


def arrival(dst, sem):
    return pltpu.make_async_copy(dst, dst, sem)


def weights_of(experts, gates, expert_count, width, first, slots):
    rows, top = experts.shape
    names = lax.broadcasted_iota(jnp.int32, (rows, expert_count), 1)
    chosen = [(experts[:, k:k + 1] == names).astype(jnp.float32) for k in range(top)]
    earlier = (
        lax.broadcasted_iota(jnp.int32, (rows, rows), 0)
        > lax.broadcasted_iota(jnp.int32, (rows, rows), 1)
    )
    before = jnp.dot(
        earlier.astype(jnp.float32).astype(jnp.bfloat16),
        sum(chosen).astype(jnp.bfloat16),
        preferred_element_type=jnp.float32,
    )
    number = lax.broadcasted_iota(jnp.int32, (rows, slots), 1) + first
    total = jnp.zeros((rows, slots), jnp.float32)
    for k in range(top):
        within = jnp.sum(chosen[k] * before, axis=1, keepdims=True).astype(jnp.int32)
        slot = experts[:, k:k + 1] * width + within
        total = total + jnp.where(number == slot, gates[:, k:k + 1], 0.0)
    high = total.astype(jnp.bfloat16)
    return high, (total - high.astype(jnp.float32)).astype(jnp.bfloat16)


def layer_kernel(
    count, depth_chunks, row_chunks, chunks,
    x, gw, uw, dw, ex, gv, out,
    own, other, gb, ub, db, dp, acc_g, acc_u, give, mine, theirs,
    outb, relayed, partial, near, far, far_ex, far_gv, w_near, w_far,
    load_sem, x_send, x_recv, h_send, h_recv, d_sem,
    m_send, m_recv, f_send, f_recv, n_send, n_recv, p_send, p_recv,
):
    e, h = lax.axis_index("expert"), lax.axis_index("helper")
    rows, width = x.shape
    slots = rows // count
    half = count // 2
    lines = half // COLUMNS
    z, y = e // COLUMNS, e % COLUMNS
    side = e // half
    place = e % half
    line = place // COLUMNS
    inner = lines - 1 + side
    is_relay = z == inner
    far_first = (1 - side) * lines
    near_slots = half * slots
    tokens = ex.shape[0]
    depth = width // depth_chunks
    part_rows = rows // row_chunks
    cols_of = width // chunks

    def load(k):
        ks = pl.ds(k * depth if isinstance(k, int) else pl.multiple_of(k * depth, depth), depth)
        return (
            pltpu.make_async_copy(x.at[:, ks], own.at[:, ks], load_sem.at[0, k]),
            pltpu.make_async_copy(gw.at[ks], gb.at[ks], load_sem.at[1, k]),
            pltpu.make_async_copy(uw.at[ks], ub.at[ks], load_sem.at[2, k]),
        )

    for k in range(depth_chunks):
        for copy in load(k):
            copy.start()
    down_load = pltpu.make_async_copy(dw, db, d_sem.at[0])
    down_load.start()

    barrier = pltpu.get_barrier_semaphore()
    for step in range(1, count):
        pl.semaphore_signal(
            barrier, inc=1, device_id={"expert": (e + step) % count}, device_id_type=MESH
        )
    pl.semaphore_signal(barrier, inc=1, device_id={"helper": 1 - h}, device_id_type=MESH)
    pl.semaphore_wait(barrier, count)

    def rows_copy(r):
        rs = pl.ds(r * part_rows, part_rows)
        return remote(x.at[rs], other.at[rs], x_send.at[r], x_recv.at[r], helper=1 - h)

    for r in range(row_chunks):
        rows_copy(r).start()
    down_copy = remote(dw, dp, d_sem.at[1], d_sem.at[2], helper=1 - h)
    down_copy.start()

    far_relay = (lines - side) * COLUMNS + y
    notes = (
        remote(ex, far_ex.at[line], m_send.at[0], m_recv.at[line, 0], expert=far_relay),
        remote(gv, far_gv.at[line], m_send.at[1], m_recv.at[line, 1], expert=far_relay),
    )
    for copy in notes:
        copy.start()

    def activate(source, first, size, target, waits):
        acc_g[pl.ds(0, size)] = jnp.zeros((size, acc_g.shape[1]), jnp.float32)
        acc_u[pl.ds(0, size)] = jnp.zeros((size, acc_u.shape[1]), jnp.float32)

        def step(k, carry):
            ks = pl.ds(pl.multiple_of(k * depth, depth), depth)
            if waits:
                for copy in load(k):
                    copy.wait()
            block = source[pl.ds(first, size), ks]
            acc_g[pl.ds(0, size)] += jnp.dot(block, gb[ks], preferred_element_type=jnp.float32)
            acc_u[pl.ds(0, size)] += jnp.dot(block, ub[ks], preferred_element_type=jnp.float32)
            return carry

        lax.fori_loop(0, depth_chunks, step, 0)
        gated = acc_g[pl.ds(0, size)]
        hidden = gated / (1.0 + jnp.exp(-gated)) * acc_u[pl.ds(0, size)]
        target[pl.ds(first, size)] = hidden.astype(jnp.bfloat16)

    activate(own, 0, rows, mine, True)

    def hidden_copy(r):
        rs = pl.ds(r * part_rows, part_rows)
        return remote(give.at[rs], theirs.at[rs], h_send.at[r], h_recv.at[r], helper=1 - h)

    for r in range(row_chunks):
        rows_copy(r).wait_recv()
        activate(other, r * part_rows, part_rows, give, False)
        hidden_copy(r).start()

    w_near[0], w_near[1] = weights_of(ex[...], gv[...], count, slots, side * near_slots, near_slots)

    down_load.wait()
    down_copy.wait_recv()
    for r in range(row_chunks):
        hidden_copy(r).wait_recv()

    def columns(c):
        return pl.ds(pl.multiple_of(c * cols_of, cols_of), cols_of)

    def rows_at(index):
        return pl.ds(pl.multiple_of(index * slots, slots), slots)

    def to_relay(c, l, step):
        column = (y + step) % COLUMNS
        block = (far_first + l) * COLUMNS + column
        source = outb.at[rows_at(block), columns(c)]
        target = relayed.at[l, rows_at(place), columns(c)]
        sem = f_recv.at[c, l, place]
        local = pltpu.make_async_copy(source, target, sem)
        away = remote(
            source, target, f_send.at[c, l, step], sem, expert=inner * COLUMNS + column
        )
        return local, away

    def to_near(c, step):
        goal = side * half + (place + step) % half
        source = outb.at[rows_at(goal), columns(c)]
        target = near.at[rows_at(place), columns(c)]
        if step == 0:
            return pltpu.make_async_copy(source, target, n_recv.at[c, place])
        return remote(source, target, n_send.at[c, step], n_recv.at[c, place], expert=goal)

    def to_far(c, l):
        goal = (far_first + l) * COLUMNS + y
        return remote(
            partial.at[l, :, columns(c)], far.at[:, columns(c)],
            p_send.at[c, l], p_recv.at[c], expert=goal,
        )

    def lower(c, carry):
        cs = columns(c)
        value = jnp.dot(mine[...], db[:, cs], preferred_element_type=jnp.float32)
        value += jnp.dot(theirs[...], dp[:, cs], preferred_element_type=jnp.float32)
        outb[:, cs] = value.astype(jnp.bfloat16)
        for l in range(lines):
            for step in range(COLUMNS):
                local, away = to_relay(c, l, step)
                if step:
                    away.start()
                else:
                    @pl.when(is_relay)
                    def _():
                        local.start()

                    @pl.when(jnp.logical_not(is_relay))
                    def _():
                        away.start()
        return carry

    lax.fori_loop(0, chunks, lower, 0)

    def send_near(c, carry):
        for step in range(half):
            to_near(c, step).start()
        return carry

    lax.fori_loop(0, chunks, send_near, 0)

    @pl.when(is_relay)
    def _():
        for l in range(lines):
            arrival(far_ex.at[l], m_recv.at[l, 0]).wait()
            arrival(far_gv.at[l], m_recv.at[l, 1]).wait()
            w_far[l, 0], w_far[l, 1] = weights_of(
                far_ex[l], far_gv[l], count, slots, side * near_slots, near_slots
            )

        def relay(c, carry):
            cs = columns(c)
            for l in range(lines):
                for s in range(half):
                    arrival(relayed.at[l, pl.ds(s * slots, slots), cs], f_recv.at[c, l, s]).wait()
                block = relayed[l, :, cs]
                value = jnp.dot(w_far[l, 0], block, preferred_element_type=jnp.float32)
                value += jnp.dot(w_far[l, 1], block, preferred_element_type=jnp.float32)
                partial[l, :, cs] = value.astype(jnp.bfloat16)
                to_far(c, l).start()
            return carry

        lax.fori_loop(0, chunks, relay, 0)

    def combine(c, carry):
        cs = columns(c)
        for s in range(half):
            arrival(near.at[pl.ds(s * slots, slots), cs], n_recv.at[c, s]).wait()
        block = near[:, cs]
        value = jnp.dot(w_near[0], block, preferred_element_type=jnp.float32)
        value += jnp.dot(w_near[1], block, preferred_element_type=jnp.float32)
        arrival(far.at[:, cs], p_recv.at[c]).wait()
        out[:, cs] = (value + far[:, cs].astype(jnp.float32)).astype(jnp.bfloat16)
        return carry

    lax.fori_loop(0, chunks, combine, 0)

    def finish(c, carry):
        for l in range(lines):
            for step in range(COLUMNS):
                away = to_relay(c, l, step)[1]
                if step:
                    away.wait_send()
                else:
                    @pl.when(jnp.logical_not(is_relay))
                    def _():
                        away.wait_send()
        for step in range(1, half):
            to_near(c, step).wait_send()

        @pl.when(is_relay)
        def _():
            for l in range(lines):
                to_far(c, l).wait_send()
        return carry

    lax.fori_loop(0, chunks, finish, 0)
    for r in range(row_chunks):
        rows_copy(r).wait_send()
        hidden_copy(r).wait_send()
    down_copy.wait_send()
    for copy in notes:
        copy.wait_send()


def fused(slot_rows, experts, gate_values, gate_weight, up_weight, down_weight):
    count = lax.axis_size("expert")
    rows, width = slot_rows.shape
    units = gate_weight.shape[2]
    tokens, top = experts.shape
    slots = rows // count
    half = count // 2
    lines = half // COLUMNS
    near_slots = half * slots
    depth_chunks, row_chunks, chunks = 4, 2, 8
    bf16, f32 = jnp.bfloat16, jnp.float32
    dma = pltpu.SemaphoreType.DMA
    vmem = pl.BlockSpec(memory_space=pltpu.VMEM)
    hbm = pl.BlockSpec(memory_space=pl.ANY)
    return pl.pallas_call(
        functools.partial(layer_kernel, count, depth_chunks, row_chunks, chunks),
        out_shape=jax.ShapeDtypeStruct((tokens, width), bf16),
        in_specs=[hbm, hbm, hbm, hbm, vmem, vmem],
        out_specs=vmem,
        scratch_shapes=[
            pltpu.VMEM((rows, width), bf16),
            pltpu.VMEM((rows, width), bf16),
            pltpu.VMEM((width, units), bf16),
            pltpu.VMEM((width, units), bf16),
            pltpu.VMEM((units, width), bf16),
            pltpu.VMEM((units, width), bf16),
            pltpu.VMEM((rows, units), f32),
            pltpu.VMEM((rows, units), f32),
            pltpu.VMEM((rows, units), bf16),
            pltpu.VMEM((rows, units), bf16),
            pltpu.VMEM((rows, units), bf16),
            pltpu.VMEM((rows, width), bf16),
            pltpu.VMEM((lines, near_slots, width), bf16),
            pltpu.VMEM((lines, tokens, width), bf16),
            pltpu.VMEM((near_slots, width), bf16),
            pltpu.VMEM((tokens, width), bf16),
            pltpu.VMEM((lines, tokens, top), jnp.int32),
            pltpu.VMEM((lines, tokens, top), f32),
            pltpu.VMEM((2, tokens, near_slots), bf16),
            pltpu.VMEM((lines, 2, tokens, near_slots), bf16),
            dma((3, depth_chunks)),
            dma((row_chunks,)), dma((row_chunks,)),
            dma((row_chunks,)), dma((row_chunks,)),
            dma((3,)),
            dma((2,)), dma((lines, 2)),
            dma((chunks, lines, COLUMNS)), dma((chunks, lines, half)),
            dma((chunks, half)), dma((chunks, half)),
            dma((chunks, lines)), dma((chunks,)),
        ],
        compiler_params=pltpu.CompilerParams(
            collective_id=0, has_side_effects=True, vmem_limit_bytes=60 << 20
        ),
        name="expert_layer",
    )(
        slot_rows,
        gate_weight.reshape(gate_weight.shape[1:]),
        up_weight.reshape(up_weight.shape[1:]),
        down_weight.reshape(down_weight.shape[1:]),
        experts,
        gate_values,
    )


def shards(slot_rows, experts, gate_values, gate_weight, up_weight, down_weight):
    tile = 16
    expert_count = lax.axis_size("expert")
    per_source = slot_rows.shape[0] // expert_count
    if per_source % tile == 0 and expert_count % (2 * COLUMNS) == 0:
        return fused(
            slot_rows, experts, gate_values, gate_weight, up_weight, down_weight
        )
    gate_part = gate_weight[0]
    up_part = up_weight[0]
    down_part = down_weight[0]
    onehot = (
        experts[:, :, None] == jnp.arange(expert_count, dtype=jnp.int32)[None, None, :]
    ).astype(jnp.int32)
    per_token = jnp.sum(onehot, axis=1)
    before = jnp.cumsum(per_token, axis=0) - per_token
    within = jnp.take_along_axis(before, experts, axis=1)
    local_slot = experts * per_source + within
    inputs = lax.all_gather(slot_rows, "helper", axis=0, tiled=True)
    gated = jnp.dot(inputs, gate_part, preferred_element_type=jnp.float32)
    lifted = jnp.dot(inputs, up_part, preferred_element_type=jnp.float32)
    hidden = (jax.nn.silu(gated) * lifted).astype(jnp.bfloat16)
    own_rows = lax.all_to_all(hidden, "helper", split_axis=0, concat_axis=1, tiled=True)
    outputs = jnp.dot(
        own_rows,
        lax.all_gather(down_part, "helper", axis=0, tiled=True),
        preferred_element_type=jnp.float32,
    ).astype(jnp.bfloat16)
    received = lax.all_to_all(outputs, "expert", split_axis=0, concat_axis=0, tiled=True)
    picked = received[local_slot]
    combined = jnp.sum(gate_values[:, :, None] * picked.astype(jnp.float32), axis=1)
    return combined.astype(jnp.bfloat16)


def solution(mesh):
    return jax.shard_map(
        shards,
        mesh=mesh,
        in_specs=(
            P(("groups", "expert", "helper"), None),
            P(("groups", "expert", "helper"), None),
            P(("groups", "expert", "helper"), None),
            P("expert", None, "helper"),
            P("expert", None, "helper"),
            P("expert", "helper", None),
        ),
        out_specs=P(("groups", "expert", "helper"), None),
        check_vma=False,
    )
```

```python
import functools
import jax
import jax.numpy as jnp
from jax import lax
from jax.experimental import pallas as pl
from jax.experimental.pallas import tpu as pltpu
from jax.sharding import PartitionSpec as P

COLUMNS = 2
MESH = pl.DeviceIdType.MESH


def remote(src, dst, send, recv, **where):
    return pltpu.make_async_remote_copy(
        src_ref=src, dst_ref=dst, send_sem=send, recv_sem=recv,
        device_id=where, device_id_type=MESH,
    )


def arrival(dst, sem):
    return pltpu.make_async_copy(dst, dst, sem)


def weights_of(experts, gates, expert_count, width, first, slots):
    top, rows = experts.shape
    names = lax.broadcasted_iota(jnp.int32, (expert_count, rows), 0)
    chosen = [(experts[k:k + 1] == names).astype(jnp.float32) for k in range(top)]
    earlier = (
        lax.broadcasted_iota(jnp.int32, (rows, rows), 0)
        < lax.broadcasted_iota(jnp.int32, (rows, rows), 1)
    )
    before = jnp.dot(
        sum(chosen).astype(jnp.bfloat16),
        earlier.astype(jnp.float32).astype(jnp.bfloat16),
        preferred_element_type=jnp.float32,
    )
    number = lax.broadcasted_iota(jnp.int32, (slots, rows), 0) + first
    total = jnp.zeros((slots, rows), jnp.float32)
    for k in range(top):
        within = jnp.sum(chosen[k] * before, axis=0, keepdims=True).astype(jnp.int32)
        slot = experts[k:k + 1] * width + within
        total = total + jnp.where(number == slot, gates[k:k + 1], 0.0)
    total = total.T
    high = total.astype(jnp.bfloat16)
    return high, (total - high.astype(jnp.float32)).astype(jnp.bfloat16)


def layer_kernel(
    count, depth_chunks, row_chunks, chunks,
    x, gw, uw, dw, ex, gv, out,
    own, other, gb, ub, db, dp, acc_g, acc_u, give, mine, theirs,
    outb, relayed, partial, near, far, far_ex, far_gv, w_near, w_far,
    load_sem, x_send, x_recv, h_send, h_recv, d_sem,
    m_send, m_recv, f_send, f_recv, n_send, n_recv, p_send, p_recv,
):
    e, h = lax.axis_index("expert"), lax.axis_index("helper")
    rows, width = x.shape
    slots = rows // count
    half = count // 2
    lines = half // COLUMNS
    z, y = e // COLUMNS, e % COLUMNS
    side = e // half
    place = e % half
    line = place // COLUMNS
    inner = lines - 1 + side
    is_relay = z == inner
    far_first = (1 - side) * lines
    near_slots = half * slots
    depth = width // depth_chunks
    part_rows = near_slots
    far_row, near_row = (1 - side) * near_slots, side * near_slots
    parts = (pl.multiple_of(far_row, 16), pl.multiple_of(near_row, 16))
    cols_of = width // chunks

    def load(k):
        ks = pl.ds(k * depth if isinstance(k, int) else pl.multiple_of(k * depth, depth), depth)
        return (
            pltpu.make_async_copy(
                x.at[pl.ds(parts[0], part_rows), ks],
                own.at[pl.ds(parts[0], part_rows), ks],
                load_sem.at[0, k],
            ),
            pltpu.make_async_copy(gw.at[ks], gb.at[ks], load_sem.at[1, k]),
            pltpu.make_async_copy(uw.at[ks], ub.at[ks], load_sem.at[2, k]),
        )

    for k in range(depth_chunks):
        for copy in load(k):
            copy.start()
    down_load = pltpu.make_async_copy(dw, db, d_sem.at[0])
    down_load.start()
    rest = pl.ds(parts[1], part_rows)
    rest_load = pltpu.make_async_copy(x.at[rest], own.at[rest], d_sem.at[3])
    rest_load.start()

    barrier = pltpu.get_barrier_semaphore()
    for step in range(1, count):
        pl.semaphore_signal(
            barrier, inc=1, device_id={"expert": (e + step) % count}, device_id_type=MESH
        )
    pl.semaphore_signal(barrier, inc=1, device_id={"helper": 1 - h}, device_id_type=MESH)
    pl.semaphore_wait(barrier, count)

    def rows_copy(r):
        rs = pl.ds(parts[r], part_rows)
        return remote(x.at[rs], other.at[rs], x_send.at[r], x_recv.at[r], helper=1 - h)

    rows_copy(0).start()
    down_copy = remote(dw, dp, d_sem.at[1], d_sem.at[2], helper=1 - h)
    down_copy.start()

    far_relay = (lines - side) * COLUMNS + y
    notes = (
        remote(ex, far_ex.at[line], m_send.at[0], m_recv.at[line, 0], expert=far_relay),
        remote(gv, far_gv.at[line], m_send.at[1], m_recv.at[line, 1], expert=far_relay),
    )
    for copy in notes:
        copy.start()

    def activate(source, first, target, waits):
        acc_g[...] = jnp.zeros_like(acc_g)
        acc_u[...] = jnp.zeros_like(acc_u)

        def step(k, carry):
            ks = pl.ds(pl.multiple_of(k * depth, depth), depth)
            if waits:
                for copy in load(k):
                    copy.wait()
            block = source[pl.ds(first, part_rows), ks]
            acc_g[...] += jnp.dot(block, gb[ks], preferred_element_type=jnp.float32)
            acc_u[...] += jnp.dot(block, ub[ks], preferred_element_type=jnp.float32)
            return carry

        lax.fori_loop(0, depth_chunks, step, 0)
        gated = acc_g[...]
        hidden = gated / (1.0 + jnp.exp(-gated)) * acc_u[...]
        target[pl.ds(first, part_rows)] = hidden.astype(jnp.bfloat16)

    def hidden_copy(r):
        rs = pl.ds(parts[r], part_rows)
        return remote(give.at[rs], theirs.at[rs], h_send.at[r], h_recv.at[r], helper=1 - h)

    def columns(c):
        return pl.ds(pl.multiple_of(c * cols_of, cols_of), cols_of)

    def rows_at(index):
        return pl.ds(pl.multiple_of(index * slots, slots), slots)

    def to_relay(c, l, step):
        column = (y + step) % COLUMNS
        block = (far_first + l) * COLUMNS + column
        source = outb.at[rows_at(block), columns(c)]
        target = relayed.at[l, rows_at(place), columns(c)]
        sem = f_recv.at[c, l, place]
        local = pltpu.make_async_copy(source, target, sem)
        away = remote(
            source, target, f_send.at[c, l, step], sem, expert=inner * COLUMNS + column
        )
        return local, away

    def to_near(c, step):
        goal = side * half + (place + step) % half
        source = outb.at[rows_at(goal), columns(c)]
        target = near.at[rows_at(place), columns(c)]
        if step == 0:
            return pltpu.make_async_copy(source, target, n_recv.at[c, place])
        return remote(source, target, n_send.at[c, step], n_recv.at[c, place], expert=goal)

    def to_far(c, l):
        goal = (far_first + l) * COLUMNS + y
        return remote(
            partial.at[l, :, columns(c)], far.at[:, columns(c)],
            p_send.at[c, l], p_recv.at[c], expert=goal,
        )

    def project(r, cs):
        rs = pl.ds(parts[r], part_rows)
        value = jnp.dot(mine[rs], db[:, cs], preferred_element_type=jnp.float32)
        value += jnp.dot(theirs[rs], dp[:, cs], preferred_element_type=jnp.float32)
        outb[rs, cs] = value.astype(jnp.bfloat16)

    activate(own, parts[0], mine, True)
    rows_copy(0).wait_recv()
    activate(other, parts[0], give, False)
    hidden_copy(0).start()
    rows_copy(1).start()
    w_near[0], w_near[1] = weights_of(ex[...], gv[...], count, slots, near_row, near_slots)
    down_load.wait()
    down_copy.wait_recv()
    hidden_copy(0).wait_recv()

    def lower(c, carry):
        project(0, columns(c))
        for l in range(lines):
            for step in range(COLUMNS):
                local, away = to_relay(c, l, step)
                if step:
                    away.start()
                else:
                    @pl.when(is_relay)
                    def _():
                        local.start()

                    @pl.when(jnp.logical_not(is_relay))
                    def _():
                        away.start()
        return carry

    lax.fori_loop(0, chunks, lower, 0)

    rest_load.wait()
    activate(own, parts[1], mine, False)
    rows_copy(1).wait_recv()
    activate(other, parts[1], give, False)
    hidden_copy(1).start()

    @pl.when(is_relay)
    def _():
        for l in range(lines):
            arrival(far_ex.at[l], m_recv.at[l, 0]).wait()
            arrival(far_gv.at[l], m_recv.at[l, 1]).wait()
            w_far[l, 0], w_far[l, 1] = weights_of(
                far_ex[l], far_gv[l], count, slots, near_row, near_slots
            )

    hidden_copy(1).wait_recv()

    def send_near(c, carry):
        project(1, columns(c))
        for step in range(half):
            to_near(c, step).start()
        return carry

    lax.fori_loop(0, chunks, send_near, 0)

    @pl.when(is_relay)
    def _():
        def relay(c, carry):
            cs = columns(c)
            for l in range(lines):
                for s in range(half):
                    arrival(relayed.at[l, pl.ds(s * slots, slots), cs], f_recv.at[c, l, s]).wait()
                block = relayed[l, :, cs]
                value = jnp.dot(w_far[l, 0], block, preferred_element_type=jnp.float32)
                value += jnp.dot(w_far[l, 1], block, preferred_element_type=jnp.float32)
                partial[l, :, cs] = value.astype(jnp.bfloat16)
                to_far(c, l).start()
            return carry

        lax.fori_loop(0, chunks, relay, 0)

    def combine(c, carry):
        cs = columns(c)
        for s in range(half):
            arrival(near.at[pl.ds(s * slots, slots), cs], n_recv.at[c, s]).wait()
        block = near[:, cs]
        value = jnp.dot(w_near[0], block, preferred_element_type=jnp.float32)
        value += jnp.dot(w_near[1], block, preferred_element_type=jnp.float32)
        arrival(far.at[:, cs], p_recv.at[c]).wait()
        out[:, cs] = (value + far[:, cs].astype(jnp.float32)).astype(jnp.bfloat16)
        return carry

    lax.fori_loop(0, chunks, combine, 0)

    def finish(c, carry):
        for l in range(lines):
            for step in range(COLUMNS):
                away = to_relay(c, l, step)[1]
                if step:
                    away.wait_send()
                else:
                    @pl.when(jnp.logical_not(is_relay))
                    def _():
                        away.wait_send()
        for step in range(1, half):
            to_near(c, step).wait_send()

        @pl.when(is_relay)
        def _():
            for l in range(lines):
                to_far(c, l).wait_send()
        return carry

    lax.fori_loop(0, chunks, finish, 0)
    for r in range(row_chunks):
        rows_copy(r).wait_send()
        hidden_copy(r).wait_send()
    down_copy.wait_send()
    for copy in notes:
        copy.wait_send()


def fused(slot_rows, experts, gate_values, gate_weight, up_weight, down_weight):
    count = lax.axis_size("expert")
    rows, width = slot_rows.shape
    units = gate_weight.shape[2]
    tokens, top = experts.shape
    slots = rows // count
    half = count // 2
    lines = half // COLUMNS
    near_slots = half * slots
    depth_chunks, row_chunks, chunks = 4, 2, 8
    bf16, f32 = jnp.bfloat16, jnp.float32
    dma = pltpu.SemaphoreType.DMA
    vmem = pl.BlockSpec(memory_space=pltpu.VMEM)
    hbm = pl.BlockSpec(memory_space=pl.ANY)
    return pl.pallas_call(
        functools.partial(layer_kernel, count, depth_chunks, row_chunks, chunks),
        out_shape=jax.ShapeDtypeStruct((tokens, width), bf16),
        in_specs=[hbm, hbm, hbm, hbm, vmem, vmem],
        out_specs=vmem,
        scratch_shapes=[
            pltpu.VMEM((rows, width), bf16),
            pltpu.VMEM((rows, width), bf16),
            pltpu.VMEM((width, units), bf16),
            pltpu.VMEM((width, units), bf16),
            pltpu.VMEM((units, width), bf16),
            pltpu.VMEM((units, width), bf16),
            pltpu.VMEM((near_slots, units), f32),
            pltpu.VMEM((near_slots, units), f32),
            pltpu.VMEM((rows, units), bf16),
            pltpu.VMEM((rows, units), bf16),
            pltpu.VMEM((rows, units), bf16),
            pltpu.VMEM((rows, width), bf16),
            pltpu.VMEM((lines, near_slots, width), bf16),
            pltpu.VMEM((lines, tokens, width), bf16),
            pltpu.VMEM((near_slots, width), bf16),
            pltpu.VMEM((tokens, width), bf16),
            pltpu.VMEM((lines, top, tokens), jnp.int32),
            pltpu.VMEM((lines, top, tokens), f32),
            pltpu.VMEM((2, tokens, near_slots), bf16),
            pltpu.VMEM((lines, 2, tokens, near_slots), bf16),
            dma((3, depth_chunks)),
            dma((row_chunks,)), dma((row_chunks,)),
            dma((row_chunks,)), dma((row_chunks,)),
            dma((4,)),
            dma((2,)), dma((lines, 2)),
            dma((chunks, lines, COLUMNS)), dma((chunks, lines, half)),
            dma((chunks, half)), dma((chunks, half)),
            dma((chunks, lines)), dma((chunks,)),
        ],
        compiler_params=pltpu.CompilerParams(
            collective_id=0, has_side_effects=True, vmem_limit_bytes=60 << 20
        ),
        name="expert_layer",
    )(
        slot_rows,
        gate_weight.reshape(gate_weight.shape[1:]),
        up_weight.reshape(up_weight.shape[1:]),
        down_weight.reshape(down_weight.shape[1:]),
        experts.T,
        gate_values.T,
    )


def shards(slot_rows, experts, gate_values, gate_weight, up_weight, down_weight):
    tile = 16
    expert_count = lax.axis_size("expert")
    per_source = slot_rows.shape[0] // expert_count
    if per_source % tile == 0 and expert_count % (2 * COLUMNS) == 0:
        return fused(
            slot_rows, experts, gate_values, gate_weight, up_weight, down_weight
        )
    gate_part = gate_weight[0]
    up_part = up_weight[0]
    down_part = down_weight[0]
    onehot = (
        experts[:, :, None] == jnp.arange(expert_count, dtype=jnp.int32)[None, None, :]
    ).astype(jnp.int32)
    per_token = jnp.sum(onehot, axis=1)
    before = jnp.cumsum(per_token, axis=0) - per_token
    within = jnp.take_along_axis(before, experts, axis=1)
    local_slot = experts * per_source + within
    inputs = lax.all_gather(slot_rows, "helper", axis=0, tiled=True)
    gated = jnp.dot(inputs, gate_part, preferred_element_type=jnp.float32)
    lifted = jnp.dot(inputs, up_part, preferred_element_type=jnp.float32)
    hidden = (jax.nn.silu(gated) * lifted).astype(jnp.bfloat16)
    own_rows = lax.all_to_all(hidden, "helper", split_axis=0, concat_axis=1, tiled=True)
    outputs = jnp.dot(
        own_rows,
        lax.all_gather(down_part, "helper", axis=0, tiled=True),
        preferred_element_type=jnp.float32,
    ).astype(jnp.bfloat16)
    received = lax.all_to_all(outputs, "expert", split_axis=0, concat_axis=0, tiled=True)
    picked = received[local_slot]
    combined = jnp.sum(gate_values[:, :, None] * picked.astype(jnp.float32), axis=1)
    return combined.astype(jnp.bfloat16)


def solution(mesh):
    return jax.shard_map(
        shards,
        mesh=mesh,
        in_specs=(
            P(("groups", "expert", "helper"), None),
            P(("groups", "expert", "helper"), None),
            P(("groups", "expert", "helper"), None),
            P("expert", None, "helper"),
            P("expert", None, "helper"),
            P("expert", "helper", None),
        ),
        out_specs=P(("groups", "expert", "helper"), None),
        check_vma=False,
    )
```

```python
import functools
import jax
import jax.numpy as jnp
from jax import lax
from jax.experimental import pallas as pl
from jax.experimental.pallas import tpu as pltpu
from jax.sharding import PartitionSpec as P

COLUMNS = 2
MESH = pl.DeviceIdType.MESH


def remote(src, dst, send, recv, **where):
    return pltpu.make_async_remote_copy(
        src_ref=src, dst_ref=dst, send_sem=send, recv_sem=recv,
        device_id=where, device_id_type=MESH,
    )


def arrival(dst, sem):
    return pltpu.make_async_copy(dst, dst, sem)


def weights_of(experts, gates, expert_count, width, first, slots):
    top, rows = experts.shape
    names = lax.broadcasted_iota(jnp.int32, (expert_count, rows), 0)
    chosen = [(experts[k:k + 1] == names).astype(jnp.float32) for k in range(top)]
    earlier = (
        lax.broadcasted_iota(jnp.int32, (rows, rows), 0)
        < lax.broadcasted_iota(jnp.int32, (rows, rows), 1)
    )
    before = jnp.dot(
        sum(chosen).astype(jnp.bfloat16),
        earlier.astype(jnp.float32).astype(jnp.bfloat16),
        preferred_element_type=jnp.float32,
    )
    number = lax.broadcasted_iota(jnp.int32, (slots, rows), 0) + first
    total = jnp.zeros((slots, rows), jnp.float32)
    for k in range(top):
        within = jnp.sum(chosen[k] * before, axis=0, keepdims=True).astype(jnp.int32)
        slot = experts[k:k + 1] * width + within
        total = total + jnp.where(number == slot, gates[k:k + 1], 0.0)
    total = total.T
    high = total.astype(jnp.bfloat16)
    return high, (total - high.astype(jnp.float32)).astype(jnp.bfloat16)


def layer_kernel(
    count, depth_chunks, row_chunks, chunks,
    x, gw, uw, dw, ex, gv, out,
    own, other, gb, ub, db, dp, acc_g, acc_u, give, mine, theirs,
    outb, relayed, partial, near, far, far_ex, far_gv, w_near, w_far,
    load_sem, x_load, x_send, x_recv, h_send, h_recv, d_sem,
    m_send, m_recv, f_send, f_recv, n_send, n_recv, p_send, p_recv,
):
    e, h = lax.axis_index("expert"), lax.axis_index("helper")
    rows, width = x.shape
    slots = rows // count
    half = count // 2
    lines = half // COLUMNS
    z, y = e // COLUMNS, e % COLUMNS
    side = e // half
    place = e % half
    line = place // COLUMNS
    inner = lines - 1 + side
    is_relay = z == inner
    far_first = (1 - side) * lines
    near_slots = half * slots
    depth = width // depth_chunks
    part_rows = near_slots
    far_row, near_row = (1 - side) * near_slots, side * near_slots
    parts = (pl.multiple_of(far_row, 16), pl.multiple_of(near_row, 16))
    cols_of = width // chunks

    def load(k):
        ks = pl.ds(k * depth if isinstance(k, int) else pl.multiple_of(k * depth, depth), depth)
        return (
            pltpu.make_async_copy(
                x.at[pl.ds(parts[0], part_rows), ks],
                own.at[pl.ds(parts[0], part_rows), ks],
                load_sem.at[0, k],
            ),
            pltpu.make_async_copy(gw.at[ks], gb.at[ks], load_sem.at[1, k]),
            pltpu.make_async_copy(uw.at[ks], ub.at[ks], load_sem.at[2, k]),
        )

    for k in range(depth_chunks):
        for copy in load(k):
            copy.start()
    rest = pl.ds(parts[1], part_rows)
    rest_load = pltpu.make_async_copy(x.at[rest], own.at[rest], x_load.at[0])

    def columns(c):
        return pl.ds(pl.multiple_of(c * cols_of, cols_of), cols_of)

    def down_load(c):
        return pltpu.make_async_copy(dw.at[:, columns(c)], db.at[:, columns(c)], d_sem.at[0, c])

    def down_copy(c):
        return remote(
            dw.at[:, columns(c)], dp.at[:, columns(c)], d_sem.at[1, c], d_sem.at[2, c],
            helper=1 - h,
        )

    def each(first, last, action):
        def step(c, carry):
            action(c)
            return carry

        lax.fori_loop(first, last, step, 0)

    barrier = pltpu.get_barrier_semaphore()
    for step in range(1, count):
        pl.semaphore_signal(
            barrier, inc=1, device_id={"expert": (e + step) % count}, device_id_type=MESH
        )
    pl.semaphore_signal(barrier, inc=1, device_id={"helper": 1 - h}, device_id_type=MESH)
    pl.semaphore_wait(barrier, count)

    def rows_copy(r):
        rs = pl.ds(parts[r], part_rows)
        return remote(x.at[rs], other.at[rs], x_send.at[r], x_recv.at[r], helper=1 - h)

    rows_copy(0).start()
    early = chunks // 2
    each(0, early, lambda c: down_copy(c).start())

    far_relay = (lines - side) * COLUMNS + y
    notes = (
        remote(ex, far_ex.at[line], m_send.at[0], m_recv.at[line, 0], expert=far_relay),
        remote(gv, far_gv.at[line], m_send.at[1], m_recv.at[line, 1], expert=far_relay),
    )
    for copy in notes:
        copy.start()

    def activate(source, first, target, waits):
        acc_g[...] = jnp.zeros_like(acc_g)
        acc_u[...] = jnp.zeros_like(acc_u)

        def step(k, carry):
            ks = pl.ds(pl.multiple_of(k * depth, depth), depth)
            if waits:
                for copy in load(k):
                    copy.wait()
            block = source[pl.ds(first, part_rows), ks]
            acc_g[...] += jnp.dot(block, gb[ks], preferred_element_type=jnp.float32)
            acc_u[...] += jnp.dot(block, ub[ks], preferred_element_type=jnp.float32)
            return carry

        lax.fori_loop(0, depth_chunks, step, 0)
        gated = acc_g[...]
        hidden = gated / (1.0 + jnp.exp(-gated)) * acc_u[...]
        target[pl.ds(first, part_rows)] = hidden.astype(jnp.bfloat16)

    def hidden_copy(r):
        rs = pl.ds(parts[r], part_rows)
        return remote(give.at[rs], theirs.at[rs], h_send.at[r], h_recv.at[r], helper=1 - h)

    def rows_at(index):
        return pl.ds(pl.multiple_of(index * slots, slots), slots)

    def to_relay(c, l, step):
        column = (y + step) % COLUMNS
        block = (far_first + l) * COLUMNS + column
        source = outb.at[rows_at(block), columns(c)]
        target = relayed.at[l, rows_at(place), columns(c)]
        sem = f_recv.at[c, l, place]
        local = pltpu.make_async_copy(source, target, sem)
        away = remote(
            source, target, f_send.at[c, l, step], sem, expert=inner * COLUMNS + column
        )
        return local, away

    def to_near(c, step):
        goal = side * half + (place + step) % half
        source = outb.at[rows_at(goal), columns(c)]
        target = near.at[rows_at(place), columns(c)]
        if step == 0:
            return pltpu.make_async_copy(source, target, n_recv.at[c, place])
        return remote(source, target, n_send.at[c, step], n_recv.at[c, place], expert=goal)

    def to_far(c, l):
        goal = (far_first + l) * COLUMNS + y
        return remote(
            partial.at[l, :, columns(c)], far.at[:, columns(c)],
            p_send.at[c, l], p_recv.at[c], expert=goal,
        )

    def project(r, cs):
        rs = pl.ds(parts[r], part_rows)
        value = jnp.dot(mine[rs], db[:, cs], preferred_element_type=jnp.float32)
        value += jnp.dot(theirs[rs], dp[:, cs], preferred_element_type=jnp.float32)
        outb[rs, cs] = value.astype(jnp.bfloat16)

    activate(own, parts[0], mine, True)
    each(0, chunks, lambda c: down_load(c).start())
    rest_load.start()
    rows_copy(0).wait_recv()
    activate(other, parts[0], give, False)
    hidden_copy(0).start()
    each(early, chunks, lambda c: down_copy(c).start())
    rows_copy(1).start()
    w_near[0], w_near[1] = weights_of(ex[...], gv[...], count, slots, near_row, near_slots)
    hidden_copy(0).wait_recv()

    def lower(c, carry):
        down_load(c).wait()
        down_copy(c).wait_recv()
        project(0, columns(c))
        for l in range(lines):
            for step in range(COLUMNS):
                local, away = to_relay(c, l, step)
                if step:
                    away.start()
                else:
                    @pl.when(is_relay)
                    def _():
                        local.start()

                    @pl.when(jnp.logical_not(is_relay))
                    def _():
                        away.start()
        return carry

    lax.fori_loop(0, chunks, lower, 0)

    rest_load.wait()
    activate(own, parts[1], mine, False)
    rows_copy(1).wait_recv()
    activate(other, parts[1], give, False)
    hidden_copy(1).start()

    @pl.when(is_relay)
    def _():
        for l in range(lines):
            arrival(far_ex.at[l], m_recv.at[l, 0]).wait()
            arrival(far_gv.at[l], m_recv.at[l, 1]).wait()
            w_far[l, 0], w_far[l, 1] = weights_of(
                far_ex[l], far_gv[l], count, slots, near_row, near_slots
            )

    hidden_copy(1).wait_recv()

    def send_near(c, carry):
        project(1, columns(c))
        for step in range(half):
            to_near(c, step).start()
        return carry

    lax.fori_loop(0, chunks, send_near, 0)

    @pl.when(is_relay)
    def _():
        def relay(c, carry):
            cs = columns(c)
            for l in range(lines):
                for s in range(half):
                    arrival(relayed.at[l, pl.ds(s * slots, slots), cs], f_recv.at[c, l, s]).wait()
                block = relayed[l, :, cs]
                value = jnp.dot(w_far[l, 0], block, preferred_element_type=jnp.float32)
                value += jnp.dot(w_far[l, 1], block, preferred_element_type=jnp.float32)
                partial[l, :, cs] = value.astype(jnp.bfloat16)
                to_far(c, l).start()
            return carry

        lax.fori_loop(0, chunks, relay, 0)

    def combine(c, carry):
        cs = columns(c)
        for s in range(half):
            arrival(near.at[pl.ds(s * slots, slots), cs], n_recv.at[c, s]).wait()
        block = near[:, cs]
        value = jnp.dot(w_near[0], block, preferred_element_type=jnp.float32)
        value += jnp.dot(w_near[1], block, preferred_element_type=jnp.float32)
        arrival(far.at[:, cs], p_recv.at[c]).wait()
        out[:, cs] = (value + far[:, cs].astype(jnp.float32)).astype(jnp.bfloat16)
        return carry

    lax.fori_loop(0, chunks, combine, 0)

    def finish(c, carry):
        for l in range(lines):
            for step in range(COLUMNS):
                away = to_relay(c, l, step)[1]
                if step:
                    away.wait_send()
                else:
                    @pl.when(jnp.logical_not(is_relay))
                    def _():
                        away.wait_send()
        for step in range(1, half):
            to_near(c, step).wait_send()

        @pl.when(is_relay)
        def _():
            for l in range(lines):
                to_far(c, l).wait_send()
        return carry

    lax.fori_loop(0, chunks, finish, 0)
    for r in range(row_chunks):
        rows_copy(r).wait_send()
        hidden_copy(r).wait_send()
    each(0, chunks, lambda c: down_copy(c).wait_send())
    for copy in notes:
        copy.wait_send()


def fused(slot_rows, experts, gate_values, gate_weight, up_weight, down_weight):
    count = lax.axis_size("expert")
    rows, width = slot_rows.shape
    units = gate_weight.shape[2]
    tokens, top = experts.shape
    slots = rows // count
    half = count // 2
    lines = half // COLUMNS
    near_slots = half * slots
    depth_chunks, row_chunks, chunks = 4, 2, 4
    bf16, f32 = jnp.bfloat16, jnp.float32
    dma = pltpu.SemaphoreType.DMA
    vmem = pl.BlockSpec(memory_space=pltpu.VMEM)
    hbm = pl.BlockSpec(memory_space=pl.ANY)
    return pl.pallas_call(
        functools.partial(layer_kernel, count, depth_chunks, row_chunks, chunks),
        out_shape=jax.ShapeDtypeStruct((tokens, width), bf16),
        in_specs=[hbm, hbm, hbm, hbm, vmem, vmem],
        out_specs=vmem,
        scratch_shapes=[
            pltpu.VMEM((rows, width), bf16),
            pltpu.VMEM((rows, width), bf16),
            pltpu.VMEM((width, units), bf16),
            pltpu.VMEM((width, units), bf16),
            pltpu.VMEM((units, width), bf16),
            pltpu.VMEM((units, width), bf16),
            pltpu.VMEM((near_slots, units), f32),
            pltpu.VMEM((near_slots, units), f32),
            pltpu.VMEM((rows, units), bf16),
            pltpu.VMEM((rows, units), bf16),
            pltpu.VMEM((rows, units), bf16),
            pltpu.VMEM((rows, width), bf16),
            pltpu.VMEM((lines, near_slots, width), bf16),
            pltpu.VMEM((lines, tokens, width), bf16),
            pltpu.VMEM((near_slots, width), bf16),
            pltpu.VMEM((tokens, width), bf16),
            pltpu.VMEM((lines, top, tokens), jnp.int32),
            pltpu.VMEM((lines, top, tokens), f32),
            pltpu.VMEM((2, tokens, near_slots), bf16),
            pltpu.VMEM((lines, 2, tokens, near_slots), bf16),
            dma((3, depth_chunks)), dma((1,)),
            dma((row_chunks,)), dma((row_chunks,)),
            dma((row_chunks,)), dma((row_chunks,)),
            dma((3, chunks)),
            dma((2,)), dma((lines, 2)),
            dma((chunks, lines, COLUMNS)), dma((chunks, lines, half)),
            dma((chunks, half)), dma((chunks, half)),
            dma((chunks, lines)), dma((chunks,)),
        ],
        compiler_params=pltpu.CompilerParams(
            collective_id=0, has_side_effects=True, vmem_limit_bytes=53 << 20
        ),
        name="expert_layer",
    )(
        slot_rows,
        gate_weight.reshape(gate_weight.shape[1:]),
        up_weight.reshape(up_weight.shape[1:]),
        down_weight.reshape(down_weight.shape[1:]),
        experts.T,
        gate_values.T,
    )


def shards(slot_rows, experts, gate_values, gate_weight, up_weight, down_weight):
    tile = 16
    expert_count = lax.axis_size("expert")
    per_source = slot_rows.shape[0] // expert_count
    if per_source % tile == 0 and expert_count % (2 * COLUMNS) == 0:
        return fused(
            slot_rows, experts, gate_values, gate_weight, up_weight, down_weight
        )
    gate_part = gate_weight[0]
    up_part = up_weight[0]
    down_part = down_weight[0]
    onehot = (
        experts[:, :, None] == jnp.arange(expert_count, dtype=jnp.int32)[None, None, :]
    ).astype(jnp.int32)
    per_token = jnp.sum(onehot, axis=1)
    before = jnp.cumsum(per_token, axis=0) - per_token
    within = jnp.take_along_axis(before, experts, axis=1)
    local_slot = experts * per_source + within
    inputs = lax.all_gather(slot_rows, "helper", axis=0, tiled=True)
    gated = jnp.dot(inputs, gate_part, preferred_element_type=jnp.float32)
    lifted = jnp.dot(inputs, up_part, preferred_element_type=jnp.float32)
    hidden = (jax.nn.silu(gated) * lifted).astype(jnp.bfloat16)
    own_rows = lax.all_to_all(hidden, "helper", split_axis=0, concat_axis=1, tiled=True)
    outputs = jnp.dot(
        own_rows,
        lax.all_gather(down_part, "helper", axis=0, tiled=True),
        preferred_element_type=jnp.float32,
    ).astype(jnp.bfloat16)
    received = lax.all_to_all(outputs, "expert", split_axis=0, concat_axis=0, tiled=True)
    picked = received[local_slot]
    combined = jnp.sum(gate_values[:, :, None] * picked.astype(jnp.float32), axis=1)
    return combined.astype(jnp.bfloat16)


def solution(mesh):
    return jax.shard_map(
        shards,
        mesh=mesh,
        in_specs=(
            P(("groups", "expert", "helper"), None),
            P(("groups", "expert", "helper"), None),
            P(("groups", "expert", "helper"), None),
            P("expert", None, "helper"),
            P("expert", None, "helper"),
            P("expert", "helper", None),
        ),
        out_specs=P(("groups", "expert", "helper"), None),
        check_vma=False,
    )
```
